32 devices in a mesh: shard: 4 (over z), ctx: 4 (over x, core), tensor: 2 (over y).
Axes of the slice: x: 2, y: 2, z: 4, core: 2. Of those that a mesh axis runs over, the one named last changes fastest.
Arguments:
- image: bfloat16 [4, 4096, 1536], P('shard', 'ctx'), may hold values from -6 to 6
- text: bfloat16 [4, 160, 1536], P('shard', 'ctx'), may hold values from -6 to 6
- cond: bfloat16 [4, 1536], P('shard'), may hold values from -6 to 6
- text_lens: int32 [4, 4], P('shard'), may hold values from 1 to 40, 154 in all within a row
- ada_weight: bfloat16 [2, 1536, 6, 1536], P(None, 'shard', None, 'tensor'), may hold values from -0.15625 to 0.15625
- ada_bias: float32 [2, 6, 1536], replicated, may hold values from -3 to 3
- qkv_weight: bfloat16 [2, 1536, 3, 1536], P(None, 'shard', None, 'tensor'), may hold values from -0.15625 to 0.15625
- proj_weight: bfloat16 [2, 1536, 1536], P(None, 'tensor', 'shard'), may hold values from -1.75 to 1.75
- fc1_weight: bfloat16 [2, 1536, 6144], P(None, 'shard', 'tensor'), may hold values from -0.15625 to 0.15625
- fc2_weight: bfloat16 [2, 6144, 1536], P(None, 'tensor', 'shard'), may hold values from -0.078125 to 0.078125
- image_cotangent: bfloat16 [4, 4096, 1536], P('shard', 'ctx'), may hold values from -6 to 6
- text_cotangent: bfloat16 [4, 160, 1536], P('shard', 'ctx'), may hold values from -6 to 6
Outputs:
- image_out: bfloat16 [4, 4096, 1536], P('shard', 'ctx')
- text_out: bfloat16 [4, 160, 1536], P('shard', 'ctx')
- image_grad: float32 [4, 4096, 1536], P('shard', 'ctx')
- text_grad: float32 [4, 160, 1536], P('shard', 'ctx')
- cond_grad: float32 [4, 1536], P('shard')
- ada_weight_grad: float32 [2, 1536, 6, 1536], P(None, 'shard', None, 'tensor')
- ada_bias_grad: float32 [2, 6, 1536], replicated
- qkv_grad: float32 [2, 1536, 3, 1536], P(None, 'shard', None, 'tensor')
- proj_grad: float32 [2, 1536, 1536], P(None, 'tensor', 'shard')
- fc1_grad: float32 [2, 1536, 6144], P(None, 'shard', 'tensor')
- fc2_grad: float32 [2, 6144, 1536], P(None, 'tensor', 'shard')
The draws below stay inside these ranges and needn't reach their ends.
Inputs may be any that keep to these rules, and one draw needn't show every extreme that they name: `text_lens`: the 4 counts of each sequence sum to 154, and one of them equals 40.
All inputs are finite; a program needn't handle non-finite values.
Results may differ from the reference program's by a relative error of at most 0.02.
The reference program's roundings to bfloat16 on the way count: a program that leaves them out, or rounds other values in their place, can miss the bound.
Values may be sent and summed in bfloat16 or wider, within the bound.
No kernel may reach another device: no remote copies, remote signals or barrier semaphores. Data moves between devices by JAX's collectives and lax.ppermute only.
A program may use at most 768 MiB of HBM per device.

```python
import math
import jax
import jax.numpy as jnp
import numpy as np
from jax import lax

D = 1536
HEADS = 24
HEAD_DIM = 64
FF = 6144
IMG = 4096
TXT = 154
TXT_DEV = 40
SEQS = 4
TXT_SLOTS = 160
N_CTX = 4


def block_levels(rng, shape, cuts, least, top_value):
    loudness = 1.0
    for dim, shards_of in cuts:
        heights = jax.random.uniform(jax.random.fold_in(jax.random.fold_in(rng, 6), dim), (shards_of,), jnp.float32, least / len(cuts), top_value / len(cuts))
        loudness = loudness * jnp.repeat(jnp.exp(heights), shape[dim] // shards_of).reshape((-1,) + (1,) * (len(shape) - 1 - dim))
    return loudness


def split_up(number_of, total, limit, skew):
    portions = [(1 << 20) // math.isqrt(grade ** skew) + 1 for grade in range(2, number_of + 1)]
    spare, counts = total - limit - (number_of - 1), [1] * (number_of - 1)
    while spare > 0:
        free = [i for i in range(number_of - 1) if counts[i] < limit]
        pool, budget = sum([portions[i] for i in free]), spare
        for i in free:
            more = min(limit - counts[i], max(1, budget * portions[i] // pool), spare)
            counts[i] = counts[i] + more
            spare = spare - more
    return np.array([limit] + counts)


def ragged(key, count, total, reach, lean):
    if count == 2:
        one = jax.random.randint(key, (), max(1, total - reach), min(reach, total - 1) + 1)
        return jnp.stack([one, total - one])
    tallies = jnp.asarray(split_up(count, total, reach, lean), jnp.int32)
    twos = (count - 1) // 2
    giver, receiver = tallies[1:1 + 2 * twos:2], tallies[2:2 + 2 * twos:2]
    margin = jnp.minimum(giver - 1, reach - receiver)
    moved = jax.random.randint(jax.random.fold_in(key, 1), (twos,), 0, 1 << 20) % (margin + 1)
    tallies = tallies.at[1:1 + 2 * twos:2].set(giver - moved).at[2:2 + 2 * twos:2].set(receiver + moved)
    return tallies[jax.random.permutation(jax.random.fold_in(key, 2), count)]


def centred(key, extent, scale, limit, split=(), kind=jnp.bfloat16):
    values = jax.random.normal(key, extent, jnp.float32) * scale
    if len(split) > 0:
        values = block_levels(key, extent, split, -0.22, 0.18) * values
    return jnp.clip(values, min=-limit, max=limit).astype(kind)


def setup_inputs(seed: int = 0) -> dict:
    seeds = jax.random.split(jax.random.key(seed), 13)
    return {
        "image": centred(seeds[0], (SEQS, IMG, D), 1.0, 6.0, ((0, 4), (1, 4))),
        "text": centred(seeds[1], (SEQS, TXT_SLOTS, D), 1.0, 6.0, ((0, 4), (1, 4))),
        "cond": centred(seeds[2], (SEQS, D), 1.0, 6.0, ((0, 4),)),
        "text_lens": jax.vmap(lambda own: ragged(own, N_CTX, TXT, TXT_DEV, 1))(jax.random.split(seeds[3], SEQS)).reshape((SEQS, N_CTX)).astype(jnp.int32),
        "ada_weight": centred(seeds[4], (2, D, 6, D), D ** -0.5, 0.15625, ((1, 4), (3, 2))),
        "ada_bias": centred(seeds[5], (2, 6, D), 0.5, 3.0, (), jnp.float32),
        "qkv_weight": centred(seeds[6], (2, D, 3, D), D ** -0.5, 0.15625, ((1, 4), (3, 2))),
        "proj_weight": centred(seeds[7], (2, D, D), (max(D // 128, 4)) ** -0.5, 1.75, ((1, 2), (2, 4))),
        "fc1_weight": centred(seeds[8], (2, D, FF), D ** -0.5, 0.15625, ((1, 4), (2, 2))),
        "fc2_weight": centred(seeds[9], (2, FF, D), FF ** -0.5, 0.078125, ((1, 2), (2, 4))),
        "image_cotangent": centred(seeds[10], (SEQS, IMG, D), 1.0, 6.0, ((0, 4), (1, 4))),
        "text_cotangent": centred(seeds[11], (SEQS, TXT_SLOTS, D), 1.0, 6.0, ((0, 4), (1, 4))),
    }


@jax.custom_vjp
def low(v):
    return lax.optimization_barrier(v.astype(jnp.bfloat16)).astype(jnp.float32)

@jax.custom_vjp
def low_back(v):
    return v

def low_keep(v):
    return (low(v), None)

def low_pass(kept, grad):
    return (grad,)

def back_keep(v):
    return (v, None)

def back_low(kept, grad):
    return (low(grad),)
low.defvjp(low_keep, low_pass)
low_back.defvjp(back_keep, back_low)
highest = lax.Precision.HIGHEST

def layer_norm(values):
    center = values - lax.optimization_barrier(jnp.mean(values, axis=-1, keepdims=True))
    spread = lax.optimization_barrier(jnp.mean(center * center, axis=-1, keepdims=True))
    return center * lax.rsqrt(spread + 1e-06)

def modulate(values, shift_vec, scale_vec):
    return layer_norm(values) * (1.0 + scale_vec) + shift_vec

def head_attention(query, key_rows, value_rows, valid):
    raw = low_back(jnp.dot(query, key_rows.T, precision=highest)) * HEAD_DIM ** (-0.5)
    scores = jnp.where(valid[None, :], raw, -jnp.inf)
    attention_weights = jax.nn.softmax(scores, axis=-1)
    return jnp.dot(low(attention_weights), value_rows, precision=highest)

def sequence_forward(image_row, text_row, cond_row, valid, ada_weight, ada_bias, qkv_weight, proj_weight, fc1_weight, fc2_weight):
    cond_low = low(jax.nn.silu(cond_row))
    modulation = jnp.einsum('e,sekf->skf', cond_low, ada_weight, precision=highest) + ada_bias
    streams = (image_row, text_row)
    packed_parts = []
    for stream in range(2):
        normed = low(modulate(streams[stream], modulation[stream, 0], modulation[stream, 1]))
        packed = jnp.einsum('re,ekf->rkf', normed, qkv_weight[stream], precision=highest)
        packed_parts.append(low(low_back(packed)))
    packed = jnp.concatenate(packed_parts, axis=0)
    total_rows = packed.shape[0]
    queries = packed[:, 0].reshape(total_rows, HEADS, HEAD_DIM).transpose(1, 0, 2)
    key_rows = packed[:, 1].reshape(total_rows, HEADS, HEAD_DIM).transpose(1, 0, 2)
    value_rows = packed[:, 2].reshape(total_rows, HEADS, HEAD_DIM).transpose(1, 0, 2)

    def one_head(items):
        return head_attention(items[0], items[1], items[2], valid)
    heads_out = lax.map(jax.checkpoint(one_head), (queries, key_rows, value_rows))
    attended = heads_out.transpose(1, 0, 2)
    attended = low(low_back(attended)).reshape(total_rows, D)
    parts = (attended[:IMG], attended[IMG:])
    results = []
    for stream in range(2):
        mods = modulation[stream]
        branch = low_back(jnp.einsum('rc,ce->re', parts[stream], proj_weight[stream], precision=highest))
        middle = streams[stream] + mods[2] * branch
        normed = low(modulate(middle, mods[3], mods[4]))
        inner = low_back(jnp.einsum('re,ef->rf', normed, fc1_weight[stream], precision=highest))
        activated = low(jax.nn.gelu(inner, approximate=True))
        mixed = low_back(jnp.einsum('rf,fe->re', activated, fc2_weight[stream], precision=highest))
        results.append(middle + mods[5] * mixed)
    return (results[0], results[1])

def reference(image, text, cond, text_lens, ada_weight, ada_bias, qkv_weight, proj_weight, fc1_weight, fc2_weight, image_cotangent, text_cotangent):
    params = tuple((matrix.astype(jnp.float32) for matrix in (ada_weight, ada_bias, qkv_weight, proj_weight, fc1_weight, fc2_weight)))
    position = jnp.arange(IMG + TXT_SLOTS, dtype=jnp.int32)
    text_pos = position - IMG
    owner = jnp.clip(text_pos // TXT_DEV, 0, N_CTX - 1).astype(jnp.int32)

    def one_sequence(totals, items):
        image_row, text_row, cond_row, lens_row, image_cot, text_cot = items
        valid = (position < IMG) | (text_pos % TXT_DEV < lens_row[owner])

        def forward(image_in, text_in, cond_in, *weights):
            return sequence_forward(image_in, text_in, cond_in, valid, *weights)
        outputs, pullback = jax.vjp(forward, image_row.astype(jnp.float32), text_row.astype(jnp.float32), cond_row.astype(jnp.float32), *params)
        grads = pullback((image_cot.astype(jnp.float32), text_cot.astype(jnp.float32)))
        totals = tuple((first + second for first, second in zip(totals, grads[3:])))
        return (totals, (outputs[0].astype(jnp.bfloat16), outputs[1].astype(jnp.bfloat16), grads[0], grads[1], grads[2]))
    start = tuple((jnp.zeros(matrix.shape, jnp.float32) for matrix in params))
    totals, per_seq = lax.scan(one_sequence, start, (image, text, cond, text_lens, image_cotangent, text_cotangent))
    return (per_seq[0], per_seq[1], per_seq[2], per_seq[3], per_seq[4], totals[0], totals[1], totals[2], totals[3], totals[4], totals[5])
```

```python
import jax
import jax.numpy as jnp
from jax import lax
from jax.experimental import pallas as pl
from jax.experimental.pallas import tpu as pltpu
from jax.sharding import PartitionSpec as P

HEAD_DIM = 64
LANES = 128
KEY_CHUNK = 512
BACK_CHUNK = 256
LOG2E = 1.4426950408889634
SCALE = HEAD_DIM ** (-0.5)

f32 = jnp.float32
bf16 = jnp.bfloat16


def dot(a, b):
    return jnp.dot(a, b, preferred_element_type=f32)


def layer_norm(values):
    center = values - jnp.mean(values, axis=-1, keepdims=True)
    spread = jnp.mean(center * center, axis=-1, keepdims=True)
    return center * lax.rsqrt(spread + 1e-06)


def modulate(values, shift_vec, scale_vec):
    return layer_norm(values) * (1.0 + scale_vec[:, None, :]) + shift_vec[:, None, :]


def gelu_tanh(values):
    return jax.nn.gelu(values, approximate=True)


def pad_rows(array, rows):
    return jnp.pad(array, ((0, rows - array.shape[0]), (0, 0)))


def pad_cols(array, cols):
    return jnp.pad(array, ((0, 0), (0, cols - array.shape[1])))


def forward_kernel(q_ref, k_ref, v_ref, kt_ref, vt_ref, bias_ref, o_ref, lse_ref):
    rows = q_ref.shape[0]
    keys = k_ref.shape[0]
    low_half = lax.broadcasted_iota(jnp.int32, (1, LANES), 1) < HEAD_DIM
    q = q_ref[...] * jnp.asarray(SCALE, bf16)
    outs = []
    for half in range(2):
        mine = low_half if half == 0 else jnp.logical_not(low_half)
        qh = jnp.where(mine, q, jnp.zeros_like(q))
        top = jnp.full((rows, 1), -jnp.inf, f32)
        acc = jnp.zeros((rows, LANES), f32)
        starts = list(range(0, keys, KEY_CHUNK)) + [None]
        for start in starts:
            if start is None:
                kc, vc = kt_ref[...], vt_ref[...]
            else:
                size = min(KEY_CHUNK, keys - start)
                kc, vc = k_ref[start : start + size], v_ref[start : start + size]
            scores = lax.dot_general(
                qh, kc, (((1,), (1,)), ((), ())), preferred_element_type=f32
            )
            if start is None:
                scores = scores + bias_ref[...]
            new_top = jnp.maximum(top, jnp.max(scores, axis=1, keepdims=True))
            probs = jnp.exp2((scores - new_top) * LOG2E)
            shrink = jnp.exp2((top - new_top) * LOG2E)
            vh = jnp.where(mine, vc, jnp.ones_like(vc))
            acc = acc * shrink + dot(probs.astype(bf16), vh)
            top = new_top
        sums = pltpu.roll(acc, HEAD_DIM, 1)
        outs.append(acc / sums)
        total = jnp.where(mine, sums, acc)
        lse = top + jnp.log(total)
        lse_ref[0, half : half + 1, :] = jnp.transpose(lse)[0:1, :]
    o_ref[...] = jnp.where(low_half, outs[0], outs[1]).astype(bf16)


def attend(q, kv, kv_text, bias, block_rows):
    rows, cols = q.shape
    keys = kv.shape[0]
    text_keys = kv_text.shape[0]
    pairs = cols // LANES
    return pl.pallas_call(
        forward_kernel,
        grid=(pairs, rows // block_rows),
        in_specs=[
            pl.BlockSpec((block_rows, LANES), lambda g, i: (i, g)),
            pl.BlockSpec((keys, LANES), lambda g, i: (0, g)),
            pl.BlockSpec((keys, LANES), lambda g, i: (0, g + pairs)),
            pl.BlockSpec((text_keys, LANES), lambda g, i: (0, g)),
            pl.BlockSpec((text_keys, LANES), lambda g, i: (0, g + pairs)),
            pl.BlockSpec((1, text_keys), lambda g, i: (0, 0)),
        ],
        out_specs=[
            pl.BlockSpec((block_rows, LANES), lambda g, i: (i, g)),
            pl.BlockSpec((1, 2, block_rows), lambda g, i: (g, 0, i)),
        ],
        out_shape=[
            jax.ShapeDtypeStruct((rows, cols), bf16),
            jax.ShapeDtypeStruct((pairs, 2, rows), f32),
        ],
        compiler_params=pltpu.CompilerParams(
            dimension_semantics=("arbitrary", "arbitrary"), vmem_limit_bytes=56 << 20
        ),
        name="attend",
    )(q, kv, kv, kv_text, kv_text, bias)


def backward_kernel(
    q_ref, do_ref, o_ref, lse_ref, k_ref, v_ref, kt_ref, vt_ref, bias_ref,
    dq_ref, dk_ref, dv_ref, dkt_ref, dvt_ref, dqt_ref,
):
    rows = q_ref.shape[0]
    keys = k_ref.shape[0]
    lane_low = lax.broadcasted_iota(jnp.int32, (1, LANES), 1) < HEAD_DIM
    row_low = lax.broadcasted_iota(jnp.int32, (LANES, 1), 0) < HEAD_DIM
    q = q_ref[...] * jnp.asarray(SCALE, bf16)
    do = do_ref[...]
    q_t = jnp.transpose(q)
    do_t = jnp.transpose(do)
    mixed_t = jnp.transpose(do.astype(f32) * o_ref[...].astype(f32))
    zero = jnp.zeros_like(q)
    zero_t = jnp.zeros_like(q_t)
    heads = []
    for half in range(2):
        mine = lane_low if half == 0 else jnp.logical_not(lane_low)
        mine_t = row_low if half == 0 else jnp.logical_not(row_low)
        part = mixed_t[half * HEAD_DIM : (half + 1) * HEAD_DIM]
        heads.append(
            (
                jnp.where(mine_t, q_t, zero_t),
                jnp.where(mine_t, do_t, zero_t),
                jnp.where(mine, q, zero),
                jnp.where(mine, do, zero),
                lse_ref[0, half : half + 1, :] * LOG2E,
                jnp.sum(part, axis=0, keepdims=True),
            )
        )
    dqt_ref[...] = jnp.zeros_like(dqt_ref)

    def chunk(kc, vc, bias):
        dk = jnp.zeros((kc.shape[0], LANES), f32)
        dv = jnp.zeros((kc.shape[0], LANES), f32)
        kc_t = jnp.transpose(kc)
        for half in range(2):
            q_th, do_th, q_h, do_h, lse, delta = heads[half]
            scores = dot(kc, q_th) * LOG2E - lse
            if bias is not None:
                scores = scores + bias
            probs = jnp.exp2(scores)
            d_probs = dot(vc, do_th)
            d_scores = (probs * (d_probs - delta)).astype(bf16)
            dv = dv + dot(probs.astype(bf16), do_h)
            dk = dk + dot(d_scores, q_h)
            span = slice(half * HEAD_DIM, (half + 1) * HEAD_DIM)
            dqt_ref[span, :] += dot(kc_t[span], d_scores)
        return dk.astype(bf16), dv.astype(bf16)

    def step(index, carry):
        at = pl.ds(pl.multiple_of(index * BACK_CHUNK, BACK_CHUNK), BACK_CHUNK)
        dk, dv = chunk(k_ref[at, :], v_ref[at, :], None)
        dk_ref[at, :] = dk
        dv_ref[at, :] = dv
        return carry

    lax.fori_loop(0, keys // BACK_CHUNK, step, 0)
    dk, dv = chunk(kt_ref[...], vt_ref[...], bias_ref[...])
    dkt_ref[...] = dk
    dvt_ref[...] = dv
    dq_ref[...] = (jnp.transpose(dqt_ref[...]) * SCALE).astype(bf16)


def attend_back(q, do, o, lse, kv, kv_text, bias_col):
    rows, cols = q.shape
    keys = kv.shape[0]
    text_keys = kv_text.shape[0]
    pairs = cols // LANES
    row_spec = pl.BlockSpec((rows, LANES), lambda g: (0, g))
    key_spec = pl.BlockSpec((keys, LANES), lambda g: (0, g))
    text_spec = pl.BlockSpec((text_keys, LANES), lambda g: (0, g))
    return pl.pallas_call(
        backward_kernel,
        grid=(pairs,),
        in_specs=[
            row_spec,
            row_spec,
            row_spec,
            pl.BlockSpec((1, 2, rows), lambda g: (g, 0, 0)),
            key_spec,
            pl.BlockSpec((keys, LANES), lambda g: (0, g + pairs)),
            text_spec,
            pl.BlockSpec((text_keys, LANES), lambda g: (0, g + pairs)),
            pl.BlockSpec((text_keys, 1), lambda g: (0, 0)),
        ],
        out_specs=[row_spec, key_spec, key_spec, text_spec, text_spec],
        out_shape=[
            jax.ShapeDtypeStruct((rows, cols), bf16),
            jax.ShapeDtypeStruct((keys, cols), bf16),
            jax.ShapeDtypeStruct((keys, cols), bf16),
            jax.ShapeDtypeStruct((text_keys, cols), bf16),
            jax.ShapeDtypeStruct((text_keys, cols), bf16),
        ],
        scratch_shapes=[pltpu.VMEM((LANES, rows), f32)],
        compiler_params=pltpu.CompilerParams(
            dimension_semantics=("arbitrary",), vmem_limit_bytes=56 << 20
        ),
        name="attend_back",
    )(q, do, o, lse, kv, kv, kv_text, kv_text, bias_col)


def tensor_sum(part):
    low = part.astype(bf16)
    if lax.axis_size("tensor") == 2:
        other = lax.ppermute(low, "tensor", [(0, 1), (1, 0)])
        return low.astype(f32) + other.astype(f32)
    return lax.psum(low, "tensor").astype(f32)


def own_quarter(array, axis):
    size = array.shape[axis] // lax.axis_size("ctx")
    return lax.dynamic_slice_in_dim(array, lax.axis_index("ctx") * size, size, axis)


def gather_rows(piece):
    return lax.all_gather(piece, ("shard", "ctx"), axis=0, tiled=True)


def reduce_rows(grad):
    piece = lax.psum_scatter(
        grad.astype(bf16), ("shard", "ctx"), scatter_dimension=0, tiled=True
    )
    return lax.all_gather(piece, "ctx", axis=0, tiled=True).astype(f32)


def ctx_sum(grad):
    return lax.psum(grad.astype(bf16), "ctx").astype(f32)


def local(
    image,
    text,
    cond,
    text_lens,
    ada_weight,
    ada_bias,
    qkv_weight,
    proj_weight,
    fc1_weight,
    fc2_weight,
    image_cotangent,
    text_cotangent,
):
    width = image.shape[2]
    image_rows = image.shape[1]
    text_rows = text.shape[1]
    local_rows = image_rows + text_rows
    cols = qkv_weight.shape[3]
    slice_rows = qkv_weight.shape[1]
    seq_index = lax.axis_index("shard")
    seqs = lax.axis_size("shard")
    ctx_count = lax.axis_size("ctx")
    col_start = lax.axis_index("tensor") * cols
    slice_start = seq_index * slice_rows

    def width_slice(array):
        return lax.dynamic_slice_in_dim(array, slice_start, slice_rows, array.ndim - 1)

    cond_all = lax.all_gather(cond, "shard", axis=0, tiled=True)
    cond_low = jax.nn.silu(cond_all.astype(f32)).astype(bf16)
    mod_part = jnp.einsum(
        "be,sekc->bskc", width_slice(cond_low), ada_weight, preferred_element_type=f32
    )
    mod_cols = lax.psum(mod_part, "shard")
    modulation_all = lax.all_gather(mod_cols, "tensor", axis=3, tiled=True) + ada_bias[None]
    modulation = lax.dynamic_slice_in_dim(modulation_all, seq_index, 1, 0)

    qkv_full = gather_rows(
        own_quarter(qkv_weight[0], 0).reshape(slice_rows // ctx_count, 3 * cols)
    )
    proj_full = gather_rows(own_quarter(proj_weight[0], 1).T)
    fc1_full = gather_rows(own_quarter(fc1_weight[0], 0))
    fc2_full = gather_rows(own_quarter(fc2_weight[0], 1).T)
    qkv_text = qkv_weight[1].reshape(slice_rows, 3 * cols)

    image_in = image.astype(f32)
    text_all = lax.all_gather(text, "shard", axis=0, tiled=True)
    text_cot_all = lax.all_gather(text_cotangent, "shard", axis=0, tiled=True).astype(f32)
    text_in = text_all.astype(f32)
    image_cot = image_cotangent.astype(f32)

    normed_a, pull_a = jax.vjp(modulate, image_in, modulation[:, 0, 0], modulation[:, 0, 1])
    low_a = normed_a.astype(bf16)[0]
    packed = dot(low_a, qkv_full).astype(bf16)
    normed_at, pull_at = jax.vjp(
        modulate, text_in, modulation_all[:, 1, 0], modulation_all[:, 1, 1]
    )
    low_at = width_slice(normed_at.astype(bf16)).reshape(seqs * text_rows, slice_rows)
    packed_text_part = dot(low_at, qkv_text).astype(bf16).reshape(seqs, text_rows, 3 * cols)
    packed_text = lax.psum_scatter(
        packed_text_part, "shard", scatter_dimension=0, tiled=True
    )[0]

    wide = -(-cols // LANES) * LANES
    query_rows = -(-local_rows // LANES) * LANES
    all_text = ctx_count * text_rows
    text_keys = -(-all_text // LANES) * LANES

    def key_columns(array):
        return jnp.concatenate(
            [pad_cols(array[:, cols : 2 * cols], wide), pad_cols(array[:, 2 * cols :], wide)],
            axis=1,
        ) if wide != cols else array[:, cols:]

    queries = pad_cols(
        pad_rows(jnp.concatenate([packed[:, :cols], packed_text[:, :cols]], axis=0), query_rows),
        wide,
    )
    kv = lax.all_gather(key_columns(packed), "ctx", axis=0, tiled=True)
    kv_text = pad_rows(
        lax.all_gather(key_columns(packed_text), "ctx", axis=0, tiled=True), text_keys
    )
    slot = jnp.arange(text_keys, dtype=jnp.int32)
    lens_at = jnp.sum(
        jnp.where(
            (slot // text_rows)[:, None] == jnp.arange(ctx_count, dtype=jnp.int32)[None, :],
            text_lens[0][None, :],
            0,
        ),
        axis=1,
    )
    valid = (slot < all_text) & (slot % text_rows < lens_at)
    bias = jnp.where(valid, 0.0, -jnp.inf).astype(f32)
    attended, lse = attend(queries, kv, kv_text, bias[None, :], query_rows // 3)
    att_image = attended[:image_rows, :cols]
    att_text = lax.all_gather(
        attended[image_rows:local_rows, :cols], "shard", axis=0, tiled=True
    )

    branch = tensor_sum(lax.dot_general(
        att_image, proj_full, (((1,), (1,)), ((), ())), preferred_element_type=f32
    ))[None]
    middle = image_in + modulation[:, 0, 2][:, None, :] * branch
    normed_m, pull_m = jax.vjp(modulate, middle, modulation[:, 0, 3], modulation[:, 0, 4])
    low_m = normed_m.astype(bf16)[0]
    inner = dot(low_m, fc1_full)
    activated, gelu_pull = jax.vjp(gelu_tanh, inner)
    act_low = activated.astype(bf16)
    mixed = tensor_sum(lax.dot_general(
        act_low, fc2_full, (((1,), (1,)), ((), ())), preferred_element_type=f32
    ))[None]
    gate_m = modulation[:, 0, 5][:, None, :]
    image_out = (middle + gate_m * mixed).astype(bf16)
    gate_m_grad = jnp.sum(image_cot * mixed, axis=1)

    d_mixed = (gate_m * image_cot).astype(bf16)[0]
    fc2_grad = reduce_rows(lax.dot_general(
        d_mixed, act_low, (((0,), (0,)), ((), ())), preferred_element_type=f32
    ))
    (d_inner,) = gelu_pull(dot(d_mixed, fc2_full))
    d_inner_low = d_inner.astype(bf16)
    fc1_grad = reduce_rows(lax.dot_general(
        low_m, d_inner_low, (((0,), (0,)), ((), ())), preferred_element_type=f32
    ))
    d_normed_m = tensor_sum(lax.dot_general(
        d_inner_low, fc1_full, (((1,), (1,)), ((), ())), preferred_element_type=f32
    ))[None]
    d_ln, shift_m_grad, scale_m_grad = pull_m(d_normed_m)
    d_middle = image_cot + d_ln
    gate_a_grad = jnp.sum(d_middle * branch, axis=1)
    d_branch = (modulation[:, 0, 2][:, None, :] * d_middle).astype(bf16)[0]
    proj_grad = reduce_rows(lax.dot_general(
        d_branch, att_image, (((0,), (0,)), ((), ())), preferred_element_type=f32
    ))
    d_att = dot(d_branch, proj_full).astype(bf16)

    def text_rows_of(part):
        total = tensor_sum(part)
        whole = lax.all_gather(total.astype(bf16), "shard", axis=1, tiled=True)
        return whole.astype(f32).reshape(seqs, text_rows, width)

    def flat(array):
        return array.reshape(seqs * text_rows, array.shape[-1])

    branch_t = text_rows_of(dot(att_text, proj_weight[1]))
    middle_t = text_in + modulation_all[:, 1, 2][:, None, :] * branch_t
    normed_mt, pull_mt = jax.vjp(
        modulate, middle_t, modulation_all[:, 1, 3], modulation_all[:, 1, 4]
    )
    low_mt = flat(width_slice(normed_mt.astype(bf16)))
    inner_t = lax.psum(dot(low_mt, fc1_weight[1]).astype(bf16), "shard").astype(f32)
    activated_t, gelu_pull_t = jax.vjp(gelu_tanh, inner_t)
    act_low_t = activated_t.astype(bf16)
    mixed_t = text_rows_of(dot(act_low_t, fc2_weight[1]))
    gate_mt = modulation_all[:, 1, 5][:, None, :]
    text_out_all = (middle_t + gate_mt * mixed_t).astype(bf16)
    gate_mt_grad = jnp.sum(text_cot_all * mixed_t, axis=1)
    d_mixed_t = flat(width_slice((gate_mt * text_cot_all).astype(bf16)))
    fc2_text_grad = ctx_sum(lax.dot_general(
        act_low_t, d_mixed_t, (((0,), (0,)), ((), ())), preferred_element_type=f32
    ))
    d_act_t = lax.psum(
        lax.dot_general(
            d_mixed_t, fc2_weight[1], (((1,), (1,)), ((), ())), preferred_element_type=f32
        ).astype(bf16),
        "shard",
    ).astype(f32)
    (d_inner_t,) = gelu_pull_t(d_act_t)
    d_inner_low_t = d_inner_t.astype(bf16)
    fc1_text_grad = ctx_sum(lax.dot_general(
        low_mt, d_inner_low_t, (((0,), (0,)), ((), ())), preferred_element_type=f32
    ))
    d_normed_mt = text_rows_of(lax.dot_general(
        d_inner_low_t, fc1_weight[1], (((1,), (1,)), ((), ())), preferred_element_type=f32
    ))
    d_ln_t, shift_mt_grad, scale_mt_grad = pull_mt(d_normed_mt)
    d_middle_t = text_cot_all + d_ln_t
    gate_at_grad = jnp.sum(d_middle_t * branch_t, axis=1)
    d_branch_t = flat(
        width_slice((modulation_all[:, 1, 2][:, None, :] * d_middle_t).astype(bf16))
    )
    proj_text_grad = ctx_sum(lax.dot_general(
        att_text, d_branch_t, (((0,), (0,)), ((), ())), preferred_element_type=f32
    ))
    d_att_text = lax.psum_scatter(
        lax.dot_general(
            d_branch_t, proj_weight[1], (((1,), (1,)), ((), ())), preferred_element_type=f32
        ).astype(bf16).reshape(seqs, text_rows, cols),
        "shard",
        scatter_dimension=0,
        tiled=True,
    )[0]

    d_attended = pad_cols(
        pad_rows(jnp.concatenate([d_att, d_att_text], axis=0), query_rows), wide
    )
    d_query, d_key, d_value, d_key_text, d_value_text = attend_back(
        queries, d_attended, attended, lse, kv, kv_text, bias[:, None]
    )
    d_kv = lax.psum_scatter(
        jnp.concatenate([d_key[:, :cols], d_value[:, :cols]], axis=1),
        "ctx", scatter_dimension=0, tiled=True,
    )
    d_kv_text = lax.psum_scatter(
        jnp.concatenate([d_key_text[:all_text, :cols], d_value_text[:all_text, :cols]], axis=1),
        "ctx", scatter_dimension=0, tiled=True,
    )
    d_packed = jnp.concatenate([d_query[:image_rows, :cols], d_kv], axis=1)
    d_packed_text = lax.all_gather(
        jnp.concatenate([d_query[image_rows:local_rows, :cols], d_kv_text], axis=1),
        "shard", axis=0, tiled=True,
    )
    qkv_grad = reduce_rows(lax.dot_general(
        low_a, d_packed, (((0,), (0,)), ((), ())), preferred_element_type=f32
    ))
    qkv_text_grad = ctx_sum(lax.dot_general(
        low_at, d_packed_text, (((0,), (0,)), ((), ())), preferred_element_type=f32
    ))
    d_normed_a = tensor_sum(lax.dot_general(
        d_packed, qkv_full, (((1,), (1,)), ((), ())), preferred_element_type=f32
    ))[None]
    d_ln, shift_a_grad, scale_a_grad = pull_a(d_normed_a)
    image_grad = d_middle + d_ln
    d_normed_at = text_rows_of(lax.dot_general(
        d_packed_text, qkv_text, (((1,), (1,)), ((), ())), preferred_element_type=f32
    ))
    d_ln_t, shift_at_grad, scale_at_grad = pull_at(d_normed_at)
    text_grad_all = d_middle_t + d_ln_t

    def own(array):
        return lax.dynamic_slice_in_dim(array, seq_index, 1, 0)

    mod_grads = jnp.stack(
        [
            jnp.concatenate(
                [shift_a_grad, scale_a_grad, gate_a_grad, shift_m_grad, scale_m_grad, gate_m_grad]
            ),
            own(
                jnp.stack(
                    [
                        shift_at_grad, scale_at_grad, gate_at_grad,
                        shift_mt_grad, scale_mt_grad, gate_mt_grad,
                    ],
                    axis=1,
                )
            )[0],
        ],
        axis=0,
    )
    mods_every = lax.all_gather(mod_grads[None], ("shard", "ctx"), axis=0, tiled=True)
    mods_seq = jnp.sum(mods_every.reshape(seqs, ctx_count, 2, 6, width), axis=1)
    bias_grad = jnp.sum(mods_seq, axis=0)
    mods_cols = lax.dynamic_slice_in_dim(mods_seq, col_start, cols, 3)
    cond_rows = width_slice(cond_low).astype(f32)
    ada_grad = sum(
        cond_rows[b][None, :, None, None] * mods_cols[b][:, None, :, :] for b in range(seqs)
    )
    ada_wide = ada_weight.astype(f32)
    d_silu_part = jnp.stack(
        [jnp.sum(ada_wide * mods_cols[b][:, None], axis=(0, 2, 3)) for b in range(seqs)]
    )
    placed = lax.dynamic_update_slice_in_dim(
        jnp.zeros((seqs, width), f32), d_silu_part, slice_start, 1
    )
    d_silu = own(lax.psum(placed, ("shard", "tensor")))
    _, silu_pull = jax.vjp(jax.nn.silu, cond.astype(f32))
    (cond_grad,) = silu_pull(d_silu)

    shape = (slice_rows, 3, cols)
    return (
        image_out,
        own(text_out_all),
        image_grad,
        own(text_grad_all),
        cond_grad,
        ada_grad,
        bias_grad,
        jnp.stack([qkv_grad.reshape(shape), qkv_text_grad.reshape(shape)]),
        jnp.stack([proj_grad.T, proj_text_grad]),
        jnp.stack([fc1_grad, fc1_text_grad]),
        jnp.stack([fc2_grad.T, fc2_text_grad]),
    )


def solution(mesh):
    return jax.shard_map(
        local,
        mesh=mesh,
        in_specs=(
            P("shard", "ctx", None),
            P("shard", "ctx", None),
            P("shard", None),
            P("shard", None),
            P(None, "shard", None, "tensor"),
            P(),
            P(None, "shard", None, "tensor"),
            P(None, "tensor", "shard"),
            P(None, "shard", "tensor"),
            P(None, "tensor", "shard"),
            P("shard", "ctx", None),
            P("shard", "ctx", None),
        ),
        out_specs=(
            P("shard", "ctx", None),
            P("shard", "ctx", None),
            P("shard", "ctx", None),
            P("shard", "ctx", None),
            P("shard", None),
            P(None, "shard", None, "tensor"),
            P(),
            P(None, "shard", None, "tensor"),
            P(None, "tensor", "shard"),
            P(None, "shard", "tensor"),
            P(None, "tensor", "shard"),
        ),
        check_vma=False,
    )
```
